32 devices in a mesh: seq: 16 (over z, x, core), head: 2 (over y).
Axes of the slice: x: 2, y: 2, z: 4, core: 2. Of those that a mesh axis runs over, the one named last changes fastest.
Arguments:
- queries: bfloat16 [8192, 3072], P(('seq', 'head'))
- keys: bfloat16 [8192, 3072], P(('seq', 'head'))
- values: bfloat16 [8192, 3072], P(('seq', 'head')), may hold values from -6 to 6
- kv_blocks: int32 [64, 64], replicated, may hold values from 0 to 63, as said below
- block_counts: int32 [64, 16], replicated, may hold values from 0 to 4, as said below
Outputs:
- attended: bfloat16 [8192, 3072], P(('seq', 'head'))
The draws below stay inside these ranges and needn't reach their ends.
Inputs may be any that keep to these rules, and one draw needn't show every extreme that they name: `kv_blocks`: slot f * 4 + j names a key block of frame f, as a global block index f * 4 + local; the valid slots of one query block and frame name distinct blocks; slots at or beyond block_counts carry a block of the same frame and no meaning. With e the distance between frame f and the frame of query block b: block_counts[b, f] is 4 where e is 0, at most 2 where e is 1, at most 1 where e is 2, 3 or a power of two, and 0 otherwise; each of these largest values is taken by the first query block of every frame.
All inputs are finite; a program needn't handle non-finite values.
Results may differ from the reference program's by a relative error of at most 0.02.
Values may be sent and summed in bfloat16 or wider, within the bound.
A program may use at most 128 MiB of HBM per device.

```python
import jax
import jax.numpy as jnp
from jax import lax

HEADS = 24
HD = 128
FTOK = 512
BLK = 128
SLOTS = 4
D = 3072
FRAMES = 16
TOKENS = 8192
QBLOCKS = 64


def block_tables(key):
    frame_blocks = FTOK // BLK
    block_ids = jnp.arange(QBLOCKS, dtype=jnp.int32)
    owner_frame = block_ids // frame_blocks
    block_place = block_ids % frame_blocks
    others = jnp.arange(FRAMES, dtype=jnp.int32)
    distance = jnp.abs(owner_frame[:, None] - others[None, :])
    power_two = (distance >= 4) & (distance & distance - 1 == 0)
    limits = jnp.where(distance == 0, SLOTS, jnp.where(distance == 1, 2, jnp.where((distance <= 3) | power_two, 1, 0))).astype(jnp.int32)
    random_counts = jax.random.randint(jax.random.fold_in(key, 13), (QBLOCKS, FRAMES), 0, 3, dtype=jnp.int32)
    counts = jnp.where(distance == 0, SLOTS, jnp.where(block_place[:, None] == 0, limits, jnp.minimum(limits, random_counts))).astype(jnp.int32)
    widths = jnp.maximum(limits, 1)
    jitter = jax.random.randint(jax.random.fold_in(key, 12), (QBLOCKS, FRAMES), 0, SLOTS, dtype=jnp.int32)
    first_block = jnp.clip(block_place[:, None] - jitter % widths, 0, frame_blocks - widths)
    slot_ids = jnp.arange(SLOTS, dtype=jnp.int32)
    offsets = jnp.where(slot_ids[None, None, :] < counts[:, :, None], slot_ids[None, None, :], 0)
    local_ids = first_block[:, :, None] + offsets
    block_lists = (others[None, :, None] * frame_blocks + local_ids).reshape(QBLOCKS, FRAMES * SLOTS)
    return (block_lists.astype(jnp.int32), counts)


def key_field(key):
    array_shape = (FRAMES * FTOK, HEADS * HD)
    return jnp.clip(jax.random.normal(jax.random.fold_in(key, 21), array_shape, jnp.float32), -6.0, 6.0)


def draw_kv_blocks(key, part):
    return block_tables(key)[0]


def draw_block_counts(key, part):
    return block_tables(key)[1]


def draw_keys(key, part):
    field_draw = key_field(key)
    return field_draw.astype(jnp.bfloat16)


def draw_queries(key, part):
    array_shape = (FRAMES * FTOK, HEADS * HD)
    return jnp.clip(2.0 * jax.random.normal(jax.random.fold_in(key, 22), array_shape, jnp.float32), -12.0, 12.0).astype(jnp.bfloat16)


def shard_levels(rng, extent, pieces, smallest, top_value):
    def one(axis_at, blocks):
        steps = jax.random.uniform(jax.random.fold_in(jax.random.fold_in(rng, 6), axis_at), (blocks,), jnp.float32, smallest / len(pieces), top_value / len(pieces))
        return jnp.repeat(jnp.exp(steps), extent[axis_at] // blocks).reshape((-1,) + (1,) * (len(extent) - axis_at - 1))

    loudness = one(*pieces[0])
    for cut in pieces[1:]:
        loudness = loudness * one(*cut)
    return loudness


def gaussian(stream_key, dims, deviation, most, shards=(), kind=jnp.bfloat16):
    array = deviation * jax.random.normal(stream_key, dims, jnp.float32)
    if shards:
        array = array * shard_levels(stream_key, dims, shards, -0.22, 0.18)
    return jnp.clip(array, -most, most).astype(kind)


def setup_inputs(seed: int = 0) -> dict:
    key_of = jax.random.split(jax.random.key(seed), 6)
    queries = draw_queries(jax.random.fold_in(key_of[5], 71), 0)
    keys = draw_keys(jax.random.fold_in(key_of[5], 71), 0)
    values = gaussian(key_of[2], (TOKENS, D), 1.0, 6.0, ((0, 32),))
    kv_blocks = draw_kv_blocks(jax.random.fold_in(key_of[5], 71), 0)
    block_counts = draw_block_counts(jax.random.fold_in(key_of[5], 71), 0)
    return dict(queries=queries, keys=keys, values=values, kv_blocks=kv_blocks, block_counts=block_counts)


NEG_FILL = -1.0e30


def rotate_time(matrix, frame_ids):
    row_count = matrix.shape[0]
    head_count = matrix.shape[1] // HD
    per_head = matrix.reshape(row_count, head_count, HD)
    pair_index = jnp.arange(8, dtype=jnp.float32)
    frequency = 256.0 ** (-pair_index / 8.0)
    angles = frame_ids.astype(jnp.float32)[:, None] * frequency[None, :]
    cosine = jnp.cos(angles)[:, None, :]
    sine_part = jnp.sin(angles)[:, None, :]
    pair_view = per_head[:, :, :16].reshape(row_count, head_count, 8, 2)
    even_part = pair_view[..., 0]
    odd_part = pair_view[..., 1]
    turned = jnp.stack([even_part * cosine - odd_part * sine_part, even_part * sine_part + odd_part * cosine], axis=-1)
    joined = jnp.concatenate([turned.reshape(row_count, head_count, 16), per_head[:, :, 16:]], axis=2)
    return joined.reshape(row_count, head_count * HD)


def signed_distances(frame_count):
    base = [1, 2, 3]
    power = 4
    while power < frame_count:
        base.append(power)
        power = power * 2
    result = [0]
    for step in base:
        result.append(step)
        result.append(-step)
    return result


def slot_cap(distance):
    if distance == 0:
        return SLOTS
    if abs(distance) == 1:
        return 2
    return 1


def frame_partial(query_group, picked_keys, picked_values, valid_counts, cap):
    scores = jnp.einsum("bqhd,bskhd->bhqsk", query_group, picked_keys.astype(jnp.float32)) * (HD ** -0.5)
    usable = (jnp.arange(cap, dtype=jnp.int32)[None, :] < valid_counts[:, None])[:, None, None, :, None]
    masked = jnp.where(usable, scores, NEG_FILL)
    part_max = jnp.max(masked, axis=(3, 4))
    probs = jnp.where(usable, jnp.exp(masked - part_max[..., None, None]), 0.0)
    part_sum = jnp.sum(probs, axis=(3, 4))
    probs_low = lax.optimization_barrier(probs.astype(jnp.bfloat16)).astype(jnp.float32)
    part_num = jnp.einsum("bhqsk,bskhd->bqhd", probs_low, picked_values.astype(jnp.float32))
    part_num = lax.optimization_barrier(part_num.astype(jnp.bfloat16)).astype(jnp.float32)
    return part_num, part_max, part_sum


def merge_state(state, part):
    run_max, run_sum, run_num = state
    part_num, part_max, part_sum = part
    new_max = jnp.maximum(run_max, part_max)
    old_scale = jnp.exp(run_max - new_max)
    new_scale = jnp.exp(part_max - new_max)
    run_sum = old_scale * run_sum + new_scale * part_sum
    run_num = run_num * jnp.transpose(old_scale, (0, 2, 1))[..., None] + part_num * jnp.transpose(new_scale, (0, 2, 1))[..., None]
    return new_max, run_sum, run_num


def reference(queries, keys, values, kv_blocks, block_counts):
    frame_blocks = FTOK // BLK
    row_frames = jnp.arange(TOKENS, dtype=jnp.int32) // FTOK
    query_turned = rotate_time(queries.astype(jnp.float32), row_frames).astype(jnp.bfloat16)
    key_turned = rotate_time(keys.astype(jnp.float32), row_frames).astype(jnp.bfloat16)
    query_all = query_turned.reshape(FRAMES, frame_blocks, BLK, HEADS, HD)
    key_blocks = key_turned.reshape(FRAMES * frame_blocks, BLK, HEADS, HD)
    value_blocks = values.reshape(FRAMES * frame_blocks, BLK, HEADS, HD)

    def one_frame(frame):
        query_group = query_all[frame].astype(jnp.float32)
        state = (jnp.full((frame_blocks, HEADS, BLK), NEG_FILL, jnp.float32), jnp.zeros((frame_blocks, HEADS, BLK), jnp.float32), jnp.zeros((frame_blocks, BLK, HEADS, HD), jnp.float32))
        for distance in signed_distances(FRAMES):
            cap = slot_cap(distance)
            source = frame - distance
            valid = (source >= 0) & (source < FRAMES)
            source_clip = jnp.clip(source, 0, FRAMES - 1).astype(jnp.int32)
            row_start = (frame * frame_blocks).astype(jnp.int32)
            block_ids = lax.dynamic_slice(kv_blocks, (row_start, (source_clip * SLOTS).astype(jnp.int32)), (frame_blocks, cap))
            counts = lax.dynamic_slice(block_counts, (row_start, source_clip), (frame_blocks, 1))[:, 0]
            counts = jnp.where(valid, counts, 0)
            part = frame_partial(query_group, key_blocks[block_ids], value_blocks[block_ids], counts, cap)
            state = merge_state(state, part)
        denominator = jnp.transpose(state[1], (0, 2, 1))[..., None]
        return state[2] / denominator

    result = lax.map(one_frame, jnp.arange(FRAMES, dtype=jnp.int32))
    return result.reshape(TOKENS, D).astype(jnp.bfloat16)
```

```python
import functools
import math

import jax
import jax.numpy as jnp
import numpy as np
from jax import lax
from jax.experimental import pallas as pl
from jax.experimental.pallas import tpu as pltpu
from jax.sharding import PartitionSpec as P

HD = 128
BLK = 128
SLOTS = 4
MESH = pl.DeviceIdType.MESH
EXP2_SCALE = HD ** (-0.5) * math.log2(math.e)


def distances(frames):
    result = [1, 2, 3]
    power = 4
    while power < frames:
        result.append(power)
        power = power * 2
    return result


def turn_table(frames):
    lane = np.arange(HD)
    frequency = (256.0 ** (-(lane // 2) / 8.0)).astype(np.float32)
    angle = np.arange(frames, dtype=np.float32)[:, None] * frequency[None, :]
    cosine = np.cos(angle.astype(np.float64))
    sine = np.sin(angle.astype(np.float64))
    turned = lane < 16
    even = lane % 2 == 0
    table = np.zeros((frames, 8, HD), np.float32)
    table[:, 0] = np.where(turned, cosine, 1.0)
    table[:, 1] = np.where(turned & even, -sine, 0.0)
    table[:, 2] = np.where(turned & ~even, sine, 0.0)
    return table


def chunk_count(heads):
    for count in (4, 3, 2):
        if heads % count == 0:
            return count
    return 1


def kernel(plan, kv_ref, count_ref, turn_ref, q_ref, k_ref, v_hbm, out_hbm, *scratch):
    frames, groups, rows, heads, chunks, offsets = plan
    width = heads // chunks * HD
    group_width = heads * HD
    chunk_heads = heads // chunks
    tokens = rows * groups
    frame_blocks = tokens // BLK
    n_off = len(offsets)
    scratch = list(scratch)

    def take(n):
        head, scratch[:] = scratch[:n], scratch[n:]
        return head

    kv = {0: take(chunks)}
    for o in offsets:
        kv[o] = take(chunks)
    q_all = take(chunks)
    att = take(chunks)
    stage_k, stage_q, scores = take(3)
    in_send, in_recv, local_sem, seq_send, seq_recv, out_send, out_recv, out_local = take(8)
    where_of = {o: i for i, o in enumerate(offsets)}

    frame = lax.axis_index("seq")
    me = lax.axis_index("head")
    core = frame % 2
    parity = (frame // 2) % 2
    sibling = frame + 1 - 2 * core
    partner = frame + 2 - 4 * parity
    my_rows = pl.ds(pl.multiple_of(me * rows, rows), rows)
    whole_blocks = rows % BLK == 0

    def rows_of(buffer, which, group):
        if whole_blocks:
            return buffer.at[which, pl.ds(group * (rows // BLK), rows // BLK)]
        first = group * rows
        return buffer.at[which, first // BLK, pl.ds(pl.multiple_of(first % BLK, rows), rows), :]

    def has(o):
        return frame + o < frames if o > 0 else frame + o >= 0

    steps = [4]
    while steps[-1] * 4 < frames:
        steps.append(steps[-1] * 2)

    barrier = pltpu.get_barrier_semaphore()

    def greet(seq, head):
        pl.semaphore_signal(barrier, inc=1, device_id=(seq, head), device_id_type=MESH)

    greet(sibling, me)
    greet(partner, me)
    expected = 2 + groups - 1
    for s in steps:
        for o in (-s, s):
            @pl.when(has(o))
            def _(o=o):
                greet(frame + o, me)

            expected = expected + jnp.where(has(o), 1, 0)
    for r in range(1, groups):
        greet(frame, (me + r) % groups)
    pl.semaphore_wait(barrier, expected)

    def turn(src, dst, column, blocked):
        table = turn_ref[frame]
        cosine, up, down = table[0:1, :], table[1:2, :], table[2:3, :]
        piece = min(rows, 32)

        @pl.loop(0, rows // piece)
        def _(i):
            at = pl.ds(pl.multiple_of(i * piece, piece), piece)
            for h in range(chunk_heads):
                col = pl.ds(pl.multiple_of(column + h * HD, HD), HD)
                x = src[at, col].astype(jnp.float32)
                y = x * cosine + pltpu.roll(x, HD - 1, 1) * up + pltpu.roll(x, 1, 1) * down
                y = y.astype(jnp.bfloat16)
                lanes = slice(h * HD, (h + 1) * HD)
                if blocked and whole_blocks:
                    inner = pl.ds(pl.multiple_of(i * piece % BLK, piece), piece)
                    dst[i * piece // BLK, inner, lanes] = y
                else:
                    dst[at, lanes] = y

    def column_of(group, c):
        return pl.multiple_of(group * group_width + c * width, HD)

    def value_columns(group, c):
        col = pl.ds(column_of(group, c), width)
        return v_hbm.at[:, :, col] if whole_blocks else v_hbm.at[:, col]

    def in_copy(c, r, what):
        target = (me + r) % groups
        if what == 0:
            src = stage_k.at[r - 1, c]
        elif what == 1:
            src = value_columns(target, c)
        else:
            src = stage_q.at[r - 1, c]
        dst = q_all[c].at[my_rows, :] if what == 2 else rows_of(kv[0][c], what, me)
        return pltpu.make_async_remote_copy(
            src_ref=src, dst_ref=dst, send_sem=in_send.at[c, r - 1, what],
            recv_sem=in_recv.at[c, r - 1, what], device_id=(frame, target), device_id_type=MESH)

    def in_wait(c, r, what):
        source = (me + groups - r) % groups
        at = pl.ds(pl.multiple_of(source * rows, rows), rows)
        dst = q_all[c].at[at, :] if what == 2 else rows_of(kv[0][c], what, source)
        pltpu.make_async_remote_copy(
            src_ref=dst, dst_ref=dst, send_sem=in_send.at[c, r - 1, what],
            recv_sem=in_recv.at[c, r - 1, what], device_id=(frame, source),
            device_id_type=MESH).wait_recv()

    def local_value(c):
        return pltpu.make_async_copy(
            value_columns(me, c), rows_of(kv[0][c], 1, me), local_sem.at[c])

    def enter(c):
        for r in range(1, groups):
            turn(k_ref, stage_k.at[r - 1, c], column_of((me + r) % groups, c), True)
            in_copy(c, r, 0).start()
            in_copy(c, r, 1).start()
        local_value(c).start()
        turn(k_ref, rows_of(kv[0][c], 0, me), column_of(me, c), True)

    def enter_queries(c):
        for r in range(1, groups):
            turn(q_ref, stage_q.at[r - 1, c], column_of((me + r) % groups, c), False)
            in_copy(c, r, 2).start()
        turn(q_ref, q_all[c].at[my_rows, :], column_of(me, c), False)

    def copy_of(c, slot, held, there, target):
        return pltpu.make_async_remote_copy(
            src_ref=kv[held][c], dst_ref=kv[there][c], send_sem=seq_send.at[c, slot],
            recv_sem=seq_recv.at[c, where_of[there]], device_id=(target, me), device_id_type=MESH)

    def wait_for(c, o, condition):
        @pl.when(condition)
        def _():
            copy_of(c, 0, o, o, sibling).wait_recv()

    even_core, odd_core = core == 0, core == 1
    low, high = parity == 0, parity == 1
    always = frame >= 0
    own_routes = [
        (has(4), 0, -4, frame + 4),
        (has(-4), 0, 4, frame - 4),
        (low, 0, -2, partner),
        (high, 0, 2, partner),
        (even_core, 0, -1, sibling),
        (odd_core, 0, 1, sibling),
    ]
    after_four = [
        (low & has(4), 4, 2, partner),
        (high & has(-4), -4, -2, partner),
        (even_core & has(4), 4, 3, sibling),
        (odd_core & has(-4), -4, -3, sibling),
    ]
    if 8 < frames:
        after_four = [
            (has(-4) & has(4), -4, -8, frame + 4),
            (has(-4) & has(4), 4, 8, frame - 4),
        ] + after_four
    after_two = [
        (low & even_core, 2, 1, sibling),
        (low & odd_core, 2, 3, sibling),
        (high & even_core, -2, -3, sibling),
        (high & odd_core, -2, -1, sibling),
    ]
    after_far_two = [
        (low & even_core & has(-2), -2, -3, sibling),
        (low & odd_core & has(-2), -2, -1, sibling),
        (high & even_core & has(2), 2, 1, sibling),
        (high & odd_core & has(2), 2, 3, sibling),
    ]
    after_power = []
    power = 8
    while power * 2 < frames:
        after_power.append((power, [
            (has(-power) & has(power), -power, -2 * power, frame + power),
            (has(-power) & has(power), power, 2 * power, frame - power),
        ]))
        power = power * 2
    routes = own_routes + after_four + after_two + after_far_two
    for _, extra in after_power:
        routes = routes + extra
    slot_of = {id(route): i for i, route in enumerate(routes)}

    def send(c, some):
        for route in some:
            condition, held, there, target = route

            @pl.when(condition)
            def _(route=route, held=held, there=there, target=target):
                copy_of(c, slot_of[id(route)], held, there, target).start()

    def send_own(c):
        for r in range(1, groups):
            in_wait(c, r, 0)
            in_wait(c, r, 1)
        local_value(c).wait()
        send(c, own_routes)

    def forward(c):
        wait_for(c, -4, has(-4))
        wait_for(c, 4, has(4))
        send(c, after_four)
        wait_for(c, 2, low)
        wait_for(c, -2, high)
        send(c, after_two)

    def forward_far(c):
        wait_for(c, -2, low & has(-2))
        wait_for(c, 2, high & has(2))
        send(c, after_far_two)
        for power, some in after_power:
            wait_for(c, -power, has(-power))
            wait_for(c, power, has(power))
            send(c, some)

    waited = [-4, 4, -2, 2]
    for power, _ in after_power:
        waited += [-power, power]

    slots = []
    for o in offsets:
        slots += [(o, j) for j in range(2 if abs(o) == 1 else 1)]
    pairs = [slots[i:i + 2] for i in range(0, len(slots), 2)]
    own_pairs = tokens // (2 * BLK)

    def attend(c):
        for o in offsets:
            if o not in waited:
                wait_for(c, o, has(o))
        for r in range(1, groups):
            in_wait(c, r, 2)

        @pl.loop(0, frame_blocks)
        def _(b):
            at = pl.ds(pl.multiple_of(b * BLK, BLK), BLK)
            table_row = frame * frame_blocks + b
            start = {}
            bound = {}
            for o, j in slots:
                there = jnp.clip(frame + o, 0, frames - 1)
                block = kv_ref[table_row, there * SLOTS + j] - there * frame_blocks
                block = jnp.clip(block, 0, frame_blocks - 1)
                start[o, j] = block
                usable = jnp.where(has(o), count_ref[table_row, there], 0) > j
                bound[o, j] = jnp.where(usable, jnp.float32(jnp.inf), jnp.float32(-jnp.inf))
            for h in range(chunk_heads):
                col = slice(h * HD, (h + 1) * HD)
                query = q_all[c][at, col]

                def side(pair, which):
                    return jnp.concatenate(
                        [kv[o][c][which, start[o, j], :, col] for o, j in pair], axis=0)

                def own_side(i, which):
                    return kv[0][c][which, 2 * i:2 * i + 2, :, col].reshape(2 * BLK, HD)

                top = None
                for i in range(own_pairs + len(pairs)):
                    if i < own_pairs:
                        key = own_side(i, 0)
                    else:
                        key = side(pairs[i - own_pairs], 0)
                    s = lax.dot_general(query, key, (((1,), (1,)), ((), ())),
                                        preferred_element_type=jnp.float32)
                    left, right = s[:, :BLK], s[:, BLK:]
                    if i >= own_pairs:
                        one, two = pairs[i - own_pairs]
                        left = jnp.minimum(left, bound[one])
                        right = jnp.minimum(right, bound[two])
                    scores[h, i, :, :BLK] = left
                    scores[h, i, :, BLK:] = right
                    both = jnp.maximum(left, right)
                    top = both if top is None else jnp.maximum(top, both)
                top = jnp.max(top, axis=1, keepdims=True)
                total = None
                out = None
                for i in range(own_pairs + len(pairs)):
                    p = jnp.exp2((scores[h, i] - top) * EXP2_SCALE)
                    part = p[:, :BLK] + p[:, BLK:]
                    total = part if total is None else total + part
                    if i < own_pairs:
                        value = own_side(i, 1)
                    else:
                        value = side(pairs[i - own_pairs], 1)
                    term = jnp.dot(p.astype(jnp.bfloat16), value, preferred_element_type=jnp.float32)
                    out = term if out is None else out + term
                total = jnp.sum(total, axis=1, keepdims=True)
                att[c][at, col] = (out / total).astype(jnp.bfloat16)

    def out_copy(c, r):
        target = (me + r) % groups
        at = pl.ds(pl.multiple_of(target * rows, rows), rows)
        return pltpu.make_async_remote_copy(
            src_ref=att[c].at[at, :], dst_ref=out_hbm.at[:, pl.ds(column_of(me, c), width)],
            send_sem=out_send.at[c, r - 1], recv_sem=out_recv.at[c, r - 1],
            device_id=(frame, target), device_id_type=MESH)

    def out_wait(c, r):
        source = (me + groups - r) % groups
        at = out_hbm.at[:, pl.ds(column_of(source, c), width)]
        pltpu.make_async_remote_copy(
            src_ref=at, dst_ref=at, send_sem=out_send.at[c, r - 1],
            recv_sem=out_recv.at[c, r - 1], device_id=(frame, source),
            device_id_type=MESH).wait_recv()

    def local_out(c):
        return pltpu.make_async_copy(
            att[c].at[my_rows, :], out_hbm.at[:, pl.ds(column_of(me, c), width)], out_local.at[c])

    def leave(c):
        for r in range(1, groups):
            out_copy(c, r).start()
        local_out(c).start()

    enter(0)
    for c in range(chunks):
        if c + 1 < chunks:
            enter(c + 1)
        send_own(c)
    for c in range(chunks):
        enter_queries(c)
    for o in offsets:
        @pl.when(jnp.logical_not(has(o)))
        def _(o=o):
            @pl.loop(0, frame_blocks)
            def _(i):
                for c in range(chunks):
                    for which in range(2):
                        kv[o][c][which, i] = jnp.zeros((BLK, width), jnp.bfloat16)

    forward(0)
    for c in range(chunks):
        if c + 1 < chunks:
            forward(c + 1)
        forward_far(c)
        attend(c)
        leave(c)

    for c in range(chunks):
        for r in range(1, groups):
            for what in range(3):
                in_copy(c, r, what).wait_send()
            out_copy(c, r).wait_send()
            out_wait(c, r)
        local_out(c).wait()
        for route in routes:
            condition, held, there, target = route

            @pl.when(condition)
            def _(route=route, held=held, there=there, target=target):
                copy_of(c, slot_of[id(route)], held, there, target).wait_send()


def local(queries, keys, values, kv_blocks, block_counts):
    frames = lax.axis_size("seq")
    groups = lax.axis_size("head")
    rows, model = queries.shape
    heads = model // HD // groups
    chunks = chunk_count(heads)
    width = heads // chunks * HD
    tokens = rows * groups
    offsets = [o for d in distances(frames) for o in (-d, d)]
    n_slots = len(offsets) + 2
    n_pairs = tokens // (2 * BLK) + n_slots // 2
    plan = (frames, groups, rows, heads, chunks, tuple(offsets))
    n_routes = 18 + 2 * len(offsets)
    lead = (rows // BLK, BLK) if rows % BLK == 0 else (rows,)
    chunk = pltpu.VMEM((2, tokens // BLK, BLK, width), jnp.bfloat16)
    flat = pltpu.VMEM((tokens, width), jnp.bfloat16)
    stage = pltpu.VMEM((max(groups - 1, 1), chunks, rows, width), jnp.bfloat16)
    stage_k = pltpu.VMEM((max(groups - 1, 1), chunks) + lead + (width,), jnp.bfloat16)
    sem = pltpu.SemaphoreType.DMA
    others = max(groups - 1, 1)
    return pl.pallas_call(
        functools.partial(kernel, plan),
        out_shape=jax.ShapeDtypeStruct((rows, model), jnp.bfloat16),
        in_specs=[
            pl.BlockSpec(memory_space=pltpu.SMEM),
            pl.BlockSpec(memory_space=pltpu.SMEM),
            pl.BlockSpec(memory_space=pltpu.VMEM),
            pl.BlockSpec(memory_space=pltpu.VMEM),
            pl.BlockSpec(memory_space=pltpu.VMEM),
            pl.BlockSpec(memory_space=pl.ANY),
        ],
        out_specs=pl.BlockSpec(memory_space=pl.ANY),
        scratch_shapes=[chunk] * (chunks * (1 + len(offsets))) + [flat] * (2 * chunks) + [
            stage_k,
            stage,
            pltpu.VMEM((heads // chunks, n_pairs, BLK, 2 * BLK), jnp.float32),
            sem((chunks, others, 3)),
            sem((chunks, others, 3)),
            sem((chunks,)),
            sem((chunks, n_routes)),
            sem((chunks, len(offsets))),
            sem((chunks, others)),
            sem((chunks, others)),
            sem((chunks,)),
        ],
        compiler_params=pltpu.CompilerParams(
            collective_id=0, has_side_effects=True, vmem_limit_bytes=60 * 1024 * 1024
        ),
    )(kv_blocks, block_counts, jnp.asarray(turn_table(frames)), queries, keys,
      values.reshape(lead + (model,)))


def solution(mesh):
    in_specs = (
        P(("seq", "head"), None),
        P(("seq", "head"), None),
        P(("seq", "head"), None),
        P(),
        P(),
    )
    out_specs = P(("seq", "head"), None)
    return jax.shard_map(local, mesh=mesh, in_specs=in_specs, out_specs=out_specs, check_vma=False)
```

```python
import functools
import math

import jax
import jax.numpy as jnp
import numpy as np
from jax import lax
from jax.experimental import pallas as pl
from jax.experimental.pallas import tpu as pltpu
from jax.sharding import PartitionSpec as P

HD = 128
BLK = 128
SLOTS = 4
MESH = pl.DeviceIdType.MESH
EXP2_SCALE = HD ** (-0.5) * math.log2(math.e)


def distances(frames):
    result = [1, 2, 3]
    power = 4
    while power < frames:
        result.append(power)
        power = power * 2
    return result


def turn_table(frames):
    lane = np.arange(HD)
    frequency = (256.0 ** (-(lane // 2) / 8.0)).astype(np.float32)
    angle = np.arange(frames, dtype=np.float32)[:, None] * frequency[None, :]
    cosine = np.cos(angle.astype(np.float64))
    sine = np.sin(angle.astype(np.float64))
    turned = lane < 16
    even = lane % 2 == 0
    table = np.zeros((frames, 8, HD), np.float32)
    table[:, 0] = np.where(turned, cosine, 1.0)
    table[:, 1] = np.where(turned & even, -sine, 0.0)
    table[:, 2] = np.where(turned & ~even, sine, 0.0)
    return table


def chunk_sizes(heads):
    if heads < 6:
        return (1,) * heads
    middle = heads - 6
    rest = (middle % 3,) if middle % 3 else ()
    return (1, 2) + (3,) * (middle // 3) + rest + (2, 1)


def kernel(plan, kv_ref, count_ref, turn_ref, q_hbm, k_hbm, v_hbm, out_hbm, *scratch):
    frames, groups, rows, heads, sizes, offsets = plan
    chunks = len(sizes)
    group_width = heads * HD
    widths = [size * HD for size in sizes]
    begins = [sum(widths[:c]) for c in range(chunks)]
    tokens = rows * groups
    frame_blocks = tokens // BLK
    n_off = len(offsets)
    scratch = list(scratch)

    def take(n):
        head, scratch[:] = scratch[:n], scratch[n:]
        return head

    kv = {0: take(chunks)}
    for o in offsets:
        kv[o] = take(chunks)
    q_all = take(chunks)
    att = take(chunks)
    q_ref, k_ref, stage_k, stage_q, scores = take(5)
    in_send, in_recv, local_sem, seq_send, seq_recv, out_send, out_recv, out_local, load_sem = take(9)
    where_of = {o: i for i, o in enumerate(offsets)}

    frame = lax.axis_index("seq")
    me = lax.axis_index("head")
    core = frame % 2
    parity = (frame // 2) % 2
    sibling = frame + 1 - 2 * core
    partner = frame + 2 - 4 * parity
    my_rows = pl.ds(pl.multiple_of(me * rows, rows), rows)
    whole_blocks = rows % BLK == 0

    def rows_of(buffer, which, group):
        if whole_blocks:
            return buffer.at[which, pl.ds(group * (rows // BLK), rows // BLK)]
        first = group * rows
        return buffer.at[which, first // BLK, pl.ds(pl.multiple_of(first % BLK, rows), rows), :]

    def has(o):
        return frame + o < frames if o > 0 else frame + o >= 0

    steps = [4]
    while steps[-1] * 4 < frames:
        steps.append(steps[-1] * 2)

    load_k = pltpu.make_async_copy(k_hbm, k_ref, load_sem.at[0])
    load_q = pltpu.make_async_copy(q_hbm, q_ref, load_sem.at[1])
    load_k.start()
    load_q.start()

    barrier = pltpu.get_barrier_semaphore()

    def greet(seq, head):
        pl.semaphore_signal(barrier, inc=1, device_id=(seq, head), device_id_type=MESH)

    greet(sibling, me)
    greet(partner, me)
    expected = 2 + groups - 1
    for s in steps:
        for o in (-s, s):
            @pl.when(has(o))
            def _(o=o):
                greet(frame + o, me)

            expected = expected + jnp.where(has(o), 1, 0)
    for r in range(1, groups):
        greet(frame, (me + r) % groups)
    pl.semaphore_wait(barrier, expected)

    def turn(src, dst, column, c, blocked):
        table = turn_ref[frame]
        cosine, up, down = table[0:1, :], table[1:2, :], table[2:3, :]
        piece = min(rows, 32)

        @pl.loop(0, rows // piece)
        def _(i):
            at = pl.ds(pl.multiple_of(i * piece, piece), piece)
            for h in range(sizes[c]):
                col = pl.ds(pl.multiple_of(column + h * HD, HD), HD)
                x = src[at, col].astype(jnp.float32)
                y = x * cosine + pltpu.roll(x, HD - 1, 1) * up + pltpu.roll(x, 1, 1) * down
                y = y.astype(jnp.bfloat16)
                lanes = slice(h * HD, (h + 1) * HD)
                if blocked and whole_blocks:
                    inner = pl.ds(pl.multiple_of(i * piece % BLK, piece), piece)
                    dst[i * piece // BLK, inner, lanes] = y
                else:
                    dst[at, lanes] = y

    def column_of(group, c):
        return pl.multiple_of(group * group_width + begins[c], HD)

    def staged(buffer, r, c, blocked):
        col = pl.ds(begins[c], widths[c])
        return buffer.at[r - 1, :, :, col] if blocked and whole_blocks else buffer.at[r - 1, :, col]

    def value_columns(group, c):
        col = pl.ds(column_of(group, c), widths[c])
        return v_hbm.at[:, :, col] if whole_blocks else v_hbm.at[:, col]

    def in_copy(c, r, what):
        target = (me + r) % groups
        if what == 0:
            src = staged(stage_k, r, c, True)
        elif what == 1:
            src = value_columns(target, c)
        else:
            src = staged(stage_q, r, c, False)
        dst = q_all[c].at[my_rows, :] if what == 2 else rows_of(kv[0][c], what, me)
        return pltpu.make_async_remote_copy(
            src_ref=src, dst_ref=dst, send_sem=in_send.at[c, r - 1, what],
            recv_sem=in_recv.at[c, r - 1, what], device_id=(frame, target), device_id_type=MESH)

    def in_wait(c, r, what):
        source = (me + groups - r) % groups
        at = pl.ds(pl.multiple_of(source * rows, rows), rows)
        dst = q_all[c].at[at, :] if what == 2 else rows_of(kv[0][c], what, source)
        pltpu.make_async_remote_copy(
            src_ref=dst, dst_ref=dst, send_sem=in_send.at[c, r - 1, what],
            recv_sem=in_recv.at[c, r - 1, what], device_id=(frame, source),
            device_id_type=MESH).wait_recv()

    def local_value(c):
        return pltpu.make_async_copy(
            value_columns(me, c), rows_of(kv[0][c], 1, me), local_sem.at[c])

    def enter(c):
        for r in range(1, groups):
            turn(k_ref, staged(stage_k, r, c, True), column_of((me + r) % groups, c), c, True)
            in_copy(c, r, 0).start()
            in_copy(c, r, 1).start()
        local_value(c).start()
        turn(k_ref, rows_of(kv[0][c], 0, me), column_of(me, c), c, True)

    def enter_queries(c):
        for r in range(1, groups):
            turn(q_ref, staged(stage_q, r, c, False), column_of((me + r) % groups, c), c, False)
            in_copy(c, r, 2).start()
        turn(q_ref, q_all[c].at[my_rows, :], column_of(me, c), c, False)

    def copy_of(c, slot, held, there, target):
        return pltpu.make_async_remote_copy(
            src_ref=kv[held][c], dst_ref=kv[there][c], send_sem=seq_send.at[c, slot],
            recv_sem=seq_recv.at[c, where_of[there]], device_id=(target, me), device_id_type=MESH)

    def wait_for(c, o, condition):
        @pl.when(condition)
        def _():
            copy_of(c, 0, o, o, sibling).wait_recv()

    even_core, odd_core = core == 0, core == 1
    low, high = parity == 0, parity == 1
    always = frame >= 0
    own_routes = [
        (has(4), 0, -4, frame + 4),
        (has(-4), 0, 4, frame - 4),
        (low, 0, -2, partner),
        (high, 0, 2, partner),
        (even_core, 0, -1, sibling),
        (odd_core, 0, 1, sibling),
    ]
    after_four = [
        (low & has(4), 4, 2, partner),
        (high & has(-4), -4, -2, partner),
        (even_core & has(4), 4, 3, sibling),
        (odd_core & has(-4), -4, -3, sibling),
    ]
    if 8 < frames:
        after_four = [
            (has(-4) & has(4), -4, -8, frame + 4),
            (has(-4) & has(4), 4, 8, frame - 4),
        ] + after_four
    after_two = [
        (low & even_core, 2, 1, sibling),
        (low & odd_core, 2, 3, sibling),
        (high & even_core, -2, -3, sibling),
        (high & odd_core, -2, -1, sibling),
    ]
    after_far_two = [
        (low & even_core & has(-2), -2, -3, sibling),
        (low & odd_core & has(-2), -2, -1, sibling),
        (high & even_core & has(2), 2, 1, sibling),
        (high & odd_core & has(2), 2, 3, sibling),
    ]
    after_power = []
    power = 8
    while power * 2 < frames:
        after_power.append((power, [
            (has(-power) & has(power), -power, -2 * power, frame + power),
            (has(-power) & has(power), power, 2 * power, frame - power),
        ]))
        power = power * 2
    routes = own_routes + after_four + after_two + after_far_two
    for _, extra in after_power:
        routes = routes + extra
    slot_of = {id(route): i for i, route in enumerate(routes)}

    def send(c, some):
        for route in some:
            condition, held, there, target = route

            @pl.when(condition)
            def _(route=route, held=held, there=there, target=target):
                copy_of(c, slot_of[id(route)], held, there, target).start()

    def send_own(c):
        for r in range(1, groups):
            in_wait(c, r, 0)
            in_wait(c, r, 1)
        local_value(c).wait()
        send(c, own_routes)

    def forward(c):
        wait_for(c, -4, has(-4))
        wait_for(c, 4, has(4))
        send(c, after_four)
        wait_for(c, 2, low)
        wait_for(c, -2, high)
        send(c, after_two)

    def forward_far(c):
        wait_for(c, -2, low & has(-2))
        wait_for(c, 2, high & has(2))
        send(c, after_far_two)
        for power, some in after_power:
            wait_for(c, -power, has(-power))
            wait_for(c, power, has(power))
            send(c, some)

    waited = [-4, 4, -2, 2]
    for power, _ in after_power:
        waited += [-power, power]

    slots = []
    for o in offsets:
        slots += [(o, j) for j in range(2 if abs(o) == 1 else 1)]
    pairs = [slots[i:i + 2] for i in range(0, len(slots), 2)]
    own_pairs = tokens // (2 * BLK)

    def attend(c):
        for o in offsets:
            if o not in waited:
                wait_for(c, o, has(o))
        for r in range(1, groups):
            in_wait(c, r, 2)

        @pl.loop(0, frame_blocks)
        def _(b):
            at = pl.ds(pl.multiple_of(b * BLK, BLK), BLK)
            table_row = frame * frame_blocks + b
            start = {}
            bound = {}
            for o, j in slots:
                there = jnp.clip(frame + o, 0, frames - 1)
                block = kv_ref[table_row, there * SLOTS + j] - there * frame_blocks
                block = jnp.clip(block, 0, frame_blocks - 1)
                start[o, j] = block
                usable = jnp.where(has(o), count_ref[there, table_row], 0) > j
                bound[o, j] = jnp.where(usable, jnp.float32(jnp.inf), jnp.float32(-jnp.inf))
            for h in range(sizes[c]):
                col = slice(h * HD, (h + 1) * HD)
                query = q_all[c][at, col]

                def side(pair, which):
                    return jnp.concatenate(
                        [kv[o][c][which, start[o, j], :, col] for o, j in pair], axis=0)

                def own_side(i, which):
                    return kv[0][c][which, 2 * i:2 * i + 2, :, col].reshape(2 * BLK, HD)

                top = None
                for i in range(own_pairs + len(pairs)):
                    if i < own_pairs:
                        key = own_side(i, 0)
                    else:
                        key = side(pairs[i - own_pairs], 0)
                    s = lax.dot_general(query, key, (((1,), (1,)), ((), ())),
                                        preferred_element_type=jnp.float32)
                    left, right = s[:, :BLK], s[:, BLK:]
                    if i >= own_pairs:
                        one, two = pairs[i - own_pairs]
                        left = jnp.minimum(left, bound[one])
                        right = jnp.minimum(right, bound[two])
                    scores[h, i, :, :BLK] = left
                    scores[h, i, :, BLK:] = right
                    both = jnp.maximum(left, right)
                    top = both if top is None else jnp.maximum(top, both)
                top = jnp.max(top, axis=1, keepdims=True)
                total = None
                out = None
                for i in range(own_pairs + len(pairs)):
                    p = jnp.exp2((scores[h, i] - top) * EXP2_SCALE)
                    part = p[:, :BLK] + p[:, BLK:]
                    total = part if total is None else total + part
                    if i < own_pairs:
                        value = own_side(i, 1)
                    else:
                        value = side(pairs[i - own_pairs], 1)
                    term = jnp.dot(p.astype(jnp.bfloat16), value, preferred_element_type=jnp.float32)
                    out = term if out is None else out + term
                total = jnp.sum(total, axis=1, keepdims=True)
                att[c][at, col] = (out / total).astype(jnp.bfloat16)

    def out_copy(c, r):
        target = (me + r) % groups
        at = pl.ds(pl.multiple_of(target * rows, rows), rows)
        return pltpu.make_async_remote_copy(
            src_ref=att[c].at[at, :], dst_ref=out_hbm.at[:, pl.ds(column_of(me, c), widths[c])],
            send_sem=out_send.at[c, r - 1], recv_sem=out_recv.at[c, r - 1],
            device_id=(frame, target), device_id_type=MESH)

    def out_wait(c, r):
        source = (me + groups - r) % groups
        at = out_hbm.at[:, pl.ds(column_of(source, c), widths[c])]
        pltpu.make_async_remote_copy(
            src_ref=at, dst_ref=at, send_sem=out_send.at[c, r - 1],
            recv_sem=out_recv.at[c, r - 1], device_id=(frame, source),
            device_id_type=MESH).wait_recv()

    def local_out(c):
        return pltpu.make_async_copy(
            att[c].at[my_rows, :], out_hbm.at[:, pl.ds(column_of(me, c), widths[c])], out_local.at[c])

    def leave(c):
        for r in range(1, groups):
            out_copy(c, r).start()
        local_out(c).start()

    load_k.wait()
    enter(0)
    for c in range(chunks):
        if c + 1 < chunks:
            enter(c + 1)
        send_own(c)
    load_q.wait()
    for c in range(chunks):
        enter_queries(c)
    for o in offsets:
        @pl.when(jnp.logical_not(has(o)))
        def _(o=o):
            @pl.loop(0, frame_blocks)
            def _(i):
                for c in range(chunks):
                    for which in range(2):
                        kv[o][c][which, i] = jnp.zeros((BLK, widths[c]), jnp.bfloat16)

    forward(0)
    for c in range(chunks):
        if c + 1 < chunks:
            forward(c + 1)
        forward_far(c)
        attend(c)
        leave(c)

    for c in range(chunks):
        for r in range(1, groups):
            for what in range(3):
                in_copy(c, r, what).wait_send()
            out_copy(c, r).wait_send()
            out_wait(c, r)
        local_out(c).wait()
        for route in routes:
            condition, held, there, target = route

            @pl.when(condition)
            def _(route=route, held=held, there=there, target=target):
                copy_of(c, slot_of[id(route)], held, there, target).wait_send()


def local(queries, keys, values, kv_blocks, block_counts):
    frames = lax.axis_size("seq")
    groups = lax.axis_size("head")
    rows, model = queries.shape
    heads = model // HD // groups
    sizes = chunk_sizes(heads)
    chunks = len(sizes)
    tokens = rows * groups
    offsets = [o for d in distances(frames) for o in (-d, d)]
    n_slots = len(offsets) + 2
    n_pairs = tokens // (2 * BLK) + n_slots // 2
    plan = (frames, groups, rows, heads, sizes, tuple(offsets))
    n_routes = 18 + 2 * len(offsets)
    lead = (rows // BLK, BLK) if rows % BLK == 0 else (rows,)
    blocks = [pltpu.VMEM((2, tokens // BLK, BLK, size * HD), jnp.bfloat16) for size in sizes]
    flats = [pltpu.VMEM((tokens, size * HD), jnp.bfloat16) for size in sizes]
    group_width = heads * HD
    whole = pltpu.VMEM((rows, model), jnp.bfloat16)
    stage_q = pltpu.VMEM((max(groups - 1, 1), rows, group_width), jnp.bfloat16)
    stage_k = pltpu.VMEM((max(groups - 1, 1),) + lead + (group_width,), jnp.bfloat16)
    sem = pltpu.SemaphoreType.DMA
    others = max(groups - 1, 1)
    return pl.pallas_call(
        functools.partial(kernel, plan),
        out_shape=jax.ShapeDtypeStruct((rows, model), jnp.bfloat16),
        in_specs=[
            pl.BlockSpec(memory_space=pltpu.SMEM),
            pl.BlockSpec(memory_space=pltpu.SMEM),
            pl.BlockSpec(memory_space=pltpu.VMEM),
            pl.BlockSpec(memory_space=pl.ANY),
            pl.BlockSpec(memory_space=pl.ANY),
            pl.BlockSpec(memory_space=pl.ANY),
        ],
        out_specs=pl.BlockSpec(memory_space=pl.ANY),
        scratch_shapes=blocks * (1 + len(offsets)) + flats * 2 + [
            whole,
            whole,
            stage_k,
            stage_q,
            pltpu.VMEM((max(sizes), n_pairs, BLK, 2 * BLK), jnp.float32),
            sem((chunks, others, 3)),
            sem((chunks, others, 3)),
            sem((chunks,)),
            sem((chunks, n_routes)),
            sem((chunks, len(offsets))),
            sem((chunks, others)),
            sem((chunks, others)),
            sem((chunks,)),
            sem((2,)),
        ],
        compiler_params=pltpu.CompilerParams(
            collective_id=0, has_side_effects=True, vmem_limit_bytes=60 * 1024 * 1024
        ),
    )(kv_blocks, block_counts.T, jnp.asarray(turn_table(frames)), queries, keys,
      values.reshape(lead + (model,)))


def solution(mesh):
    in_specs = (
        P(("seq", "head"), None),
        P(("seq", "head"), None),
        P(("seq", "head"), None),
        P(),
        P(),
    )
    out_specs = P(("seq", "head"), None)
    return jax.shard_map(local, mesh=mesh, in_specs=in_specs, out_specs=out_specs, check_vma=False)
```
